768 devices in a mesh: section: 96 (over z, y), head: 8 (over x, core).
Axes of the slice: x: 4, y: 8, z: 12, core: 2. Of those that a mesh axis runs over, the one named last changes fastest.
Arguments:
- queries: bfloat16 [24576, 8192], P('section', 'head'), may hold values from -40 to 40
- new_keys: bfloat16 [24576, 1024], P('section', 'head'), may hold values from -6 to 6
- new_values: bfloat16 [24576, 1024], P('section', 'head'), may hold values from -6 to 6
- cache_keys: bfloat16 [96, 8, 768, 128], P('section', 'head'), may hold values from -6 to 6
- cache_values: bfloat16 [96, 8, 768, 128], P('section', 'head'), may hold values from -6 to 6
- key_counts: int32 [96], replicated, may hold values from 1 to 768, 36864 in all
- scale_exps: int32 [96, 2], replicated, may hold values from -2 to 2
- out_weight: bfloat16 [8192, 4096], P('head'), may hold values from -0.0625 to 0.0625
Outputs:
- handed: float32 [24576, 4096], P(('section', 'head'))
The draws below stay inside these ranges and needn't reach their ends.
Inputs may be any that keep to these rules, and one draw needn't show every extreme that they name: `key_counts`: some section holds exactly 768 live slots, and the counts sum to 36864.
All inputs are finite; a program needn't handle non-finite values.
Results may differ from the reference program's by a relative error of at most 0.023.
Values may be sent and summed in bfloat16 or wider, within the bound.
No kernel may reach another device: no remote copies, remote signals or barrier semaphores. Data moves between devices by JAX's collectives and lax.ppermute only.
A program may use at most 64 MiB of HBM per device.

```python
import math
import jax
import jax.numpy as jnp
import numpy as np
from jax import lax

QHEADS = 64
KV_HEADS = 8
HD = 128
OUTW = 4096
ROWS = 256
CACHE_MAX = 768
GROUP = 8
SECTIONS = 96
TOKENS = 24576
N_HEAD = 8


def draw_queries(key, part):
    shape = (TOKENS, QHEADS * HD)
    values = jnp.clip(jax.random.normal(key, shape, jnp.float32), -4.0, 4.0)
    return values.astype(jnp.bfloat16)


def set_ends(drawn, stream_key, least, top_value):
    longest = drawn.shape.index(max(drawn.shape))
    spots = []
    for shift in (0, 1):
        where = [jax.random.randint(jax.random.fold_in(stream_key, axis), (), 0, length) for axis, length in enumerate(drawn.shape)]
        where[longest] = (where[longest] + shift) % drawn.shape[longest]
        spots.append(tuple(where))
    return drawn.at[spots[0]].set(least).at[spots[1]].set(top_value)


def steps_of(own_key, dims, shards, low, top_value):
    def one(dim, shards_of):
        heights = jax.random.uniform(jax.random.fold_in(jax.random.fold_in(own_key, 6), dim), (shards_of,), jnp.float32, low / len(shards), top_value / len(shards))
        return jnp.repeat(jnp.exp(heights), dims[dim] // shards_of).reshape((-1,) + (1,) * (len(dims) - dim - 1))

    gain = one(*shards[0])
    for cut in shards[1:]:
        gain = gain * one(*cut)
    return gain


def split_up(amount, total, reach, slope):
    loads = [(1 << 20) // math.isqrt(grade ** slope) + 1 for grade in range(2, amount + 1)]
    spare, holding = total - reach - (amount - 1), [1] * (amount - 1)
    while spare > 0:
        candidates = [i for i in range(amount - 1) if holding[i] < reach]
        pool, budget = sum([loads[i] for i in candidates]), spare
        for i in candidates:
            more = min(reach - holding[i], max(1, budget * loads[i] // pool), spare)
            holding[i] = holding[i] + more
            spare = spare - more
    return np.array([reach] + holding)


def uneven(key, amount, total, limit, slope):
    if amount == 2:
        one = jax.random.randint(key, (), max(1, total - limit), min(limit, total - 1) + 1)
        return jnp.stack([one, total - one])
    sizes = jnp.asarray(split_up(amount, total, limit, slope), jnp.int32)
    couples = (amount - 1) // 2
    giver, sink = sizes[1:1 + 2 * couples:2], sizes[2:2 + 2 * couples:2]
    slack = jnp.minimum(giver - 1, limit - sink)
    shifted = jax.random.randint(jax.random.fold_in(key, 1), (couples,), 0, 1 << 20) % (slack + 1)
    sizes = sizes.at[1:1 + 2 * couples:2].set(giver - shifted).at[2:2 + 2 * couples:2].set(sink + shifted)
    return sizes[jax.random.permutation(jax.random.fold_in(key, 2), amount)]


def bell_draw(own_key, extent, scale, most, cuts=(), kind=jnp.bfloat16):
    array = scale * jax.random.normal(own_key, extent, jnp.float32)
    if cuts:
        array = array * steps_of(own_key, extent, cuts, -0.22, 0.18)
    return jnp.clip(array, -most, most).astype(kind)


def setup_inputs(seed: int = 0) -> dict:
    splits = jax.random.split(jax.random.key(seed), 9)
    queries = draw_queries(jax.random.fold_in(splits[8], 71), 0)
    new_keys = bell_draw(splits[1], (TOKENS, KV_HEADS * HD), 1.0, 6.0, ((0, 96), (1, 8)))
    new_values = bell_draw(splits[2], (TOKENS, KV_HEADS * HD), 1.0, 6.0, ((0, 96), (1, 8)))
    cache_keys = bell_draw(splits[3], (SECTIONS, KV_HEADS, CACHE_MAX, HD), 1.0, 6.0, ((0, 96), (1, 8)))
    cache_values = bell_draw(splits[4], (SECTIONS, KV_HEADS, CACHE_MAX, HD), 1.0, 6.0, ((0, 96), (1, 8)))
    key_counts = uneven(splits[5], SECTIONS, SECTIONS * CACHE_MAX // 2, CACHE_MAX, 2).astype(jnp.int32)
    scale_exps = set_ends(jax.random.randint(splits[6], (SECTIONS, 2), -2, 3), jax.random.fold_in(splits[6], 1), -2, 2).astype(jnp.int32)
    out_weight = bell_draw(splits[7], (QHEADS * HD, OUTW), (QHEADS * HD) ** -0.5, 0.0625, ((0, 8),))
    return {"queries": queries, "new_keys": new_keys, "new_values": new_values, "cache_keys": cache_keys, "cache_values": cache_values, "key_counts": key_counts, "scale_exps": scale_exps, "out_weight": out_weight}


def partial_block(query_heads, key_block, value_block, visible, key_scale, value_scale):
    scores = jnp.einsum('rkgh,kch->rkgc', query_heads.astype(jnp.float32), key_block.astype(jnp.float32))
    scores = scores * (key_scale / math.sqrt(query_heads.shape[-1]))
    scores = jnp.where(visible, scores, -1e+30)
    row_peak = lax.optimization_barrier(jnp.max(scores, axis=-1))
    weights = jnp.where(visible, jnp.exp(scores - row_peak[..., None]), 0.0)
    row_total = lax.optimization_barrier(jnp.sum(weights, axis=-1))
    rounded = lax.optimization_barrier(weights.astype(jnp.bfloat16))
    summed = jnp.einsum('rkgc,kch->rkgh', rounded.astype(jnp.float32), value_block.astype(jnp.float32)) * value_scale
    summed = lax.optimization_barrier(summed.astype(jnp.bfloat16))
    return (summed, row_peak, row_total)

def merge_blocks(pieces):
    peaks = jnp.stack([piece[1] for piece in pieces])
    top_peak = lax.optimization_barrier(jnp.max(peaks, axis=0))
    factors = jnp.exp(peaks - top_peak[None])
    numer = sum((factors[n][..., None] * pieces[n][0].astype(jnp.float32) for n in range(len(pieces))))
    denom = sum((factors[n] * pieces[n][2] for n in range(len(pieces))))
    return numer / denom[..., None]

def reference(queries, new_keys, new_values, cache_keys, cache_values, key_counts, scale_exps, out_weight):
    slots = jnp.arange(CACHE_MAX, dtype=jnp.int32)
    positions = jnp.arange(ROWS, dtype=jnp.int32)
    causal = (positions[:, None] >= positions[None, :])[:, None, None, :]
    grouped = out_weight.reshape(N_HEAD, -1, OUTW).astype(jnp.float32)

    def one_section(section_pos):
        start = section_pos * ROWS
        query_rows = lax.dynamic_slice_in_dim(queries, start, ROWS, 0).reshape(ROWS, KV_HEADS, GROUP, HD)
        fresh_keys = lax.dynamic_slice_in_dim(new_keys, start, ROWS, 0).reshape(ROWS, KV_HEADS, HD).transpose(1, 0, 2)
        fresh_values = lax.dynamic_slice_in_dim(new_values, start, ROWS, 0).reshape(ROWS, KV_HEADS, HD).transpose(1, 0, 2)
        pieces = [partial_block(query_rows, fresh_keys, fresh_values, causal, 1.0, 1.0)]
        for distance in (0, 1, 2):
            index = section_pos - distance
            source = jnp.maximum(index, 0).astype(jnp.int32)
            visible = ((slots < key_counts[source]) & (index >= 0))[None, None, None, :]
            key_scale = jnp.exp2(scale_exps[source, 0].astype(jnp.float32))
            value_scale = jnp.exp2(scale_exps[source, 1].astype(jnp.float32))
            pieces.append(partial_block(query_rows, cache_keys[source], cache_values[source], visible, key_scale, value_scale))
        attended = merge_blocks(pieces).astype(jnp.bfloat16).reshape(ROWS, N_HEAD, -1)
        partials = jnp.einsum('rnc,nco->nro', attended.astype(jnp.float32), grouped)
        return lax.optimization_barrier(jnp.sum(partials, axis=0))
    projected = lax.map(one_section, jnp.arange(SECTIONS, dtype=jnp.int32)).reshape(TOKENS, OUTW)
    return jnp.roll(projected, ROWS, axis=0)
```

```python
import functools
import math

import jax
import jax.numpy as jnp
from jax import lax
from jax.experimental import pallas as pl
from jax.experimental.pallas import tpu as pltpu
from jax.sharding import PartitionSpec as P


HD = 128
GROUP = 8
MASKED = -1e30
LOG2E = 1.4426950408889634
BASE_FACTOR = LOG2E / math.sqrt(HD)
CHUNK = 256
ONES_ROWS = 16

VMEM = pl.BlockSpec(memory_space=pltpu.VMEM)
HBM = pl.BlockSpec(memory_space=pltpu.HBM)


def cache_facts(counts_ref, exps_ref, distance, width):
    index = lax.axis_index("section") - distance
    source = jnp.maximum(index, 0)
    live = jnp.full((1, width), jnp.where(index >= 0, counts_ref[source], 0), jnp.int32)
    key_exp = jnp.full((1, width), exps_ref[0, source], jnp.int32).astype(jnp.float32)
    value_exp = jnp.full((1, width), exps_ref[1, source], jnp.int32).astype(jnp.float32)
    return live, jnp.exp2(key_exp) * BASE_FACTOR, jnp.exp2(value_exp)


def facts_at(live_ref, scale_ref, distance):
    return (
        live_ref[distance : distance + 1, :],
        scale_ref[2 * distance : 2 * distance + 1, :],
        scale_ref[2 * distance + 1 : 2 * distance + 2, :],
    )


def fold_max(block):
    top = block[0:8]
    for at in range(8, block.shape[0], 8):
        top = jnp.maximum(top, block[at : at + 8])
    return top


def scores_of(key_block, q_ref, head):
    q = q_ref[:, head * HD : (head + 1) * HD]
    return lax.dot_general(key_block, q, (((1,), (1,)), ((), ())), preferred_element_type=jnp.float32)


def cache_scores(k_ref, q_ref, head, at, live):
    scores = scores_of(k_ref[at : at + CHUNK, :], q_ref, head)
    visible = lax.broadcasted_iota(jnp.int32, (CHUNK, HD), 0) < live[:, :HD] - at
    return jnp.concatenate(
        [jnp.where(visible, scores[:, n : n + HD], MASKED) for n in range(0, scores.shape[1], HD)], axis=1
    )


def fill_values(v_ref, vt_ref):
    vt_ref[:HD, :] = v_ref[...].T
    vt_ref[HD:, :] = jnp.ones((ONES_ROWS, vt_ref.shape[1]), jnp.bfloat16)


def own_kernel(
    counts_hbm, exps_hbm, q_hbm, nk_hbm, nv_hbm, k_hbm, v_hbm,
    acc_ref, peak_ref, total_ref, q_ref, live_ref, scale_ref,
    counts_ref, exps_ref, nk_ref, nv_ref, k_ref, v_ref,
    vt_ref, nvt_ref, s_ref, n_ref, p_ref, pn_ref, sems,
):
    pairs = (
        (counts_hbm, counts_ref), (exps_hbm, exps_ref), (q_hbm, q_ref), (nk_hbm, nk_ref),
        (k_hbm, k_ref), (nv_hbm, nv_ref), (v_hbm, v_ref),
    )
    copies = [pltpu.make_async_copy(source, target, sems.at[n]) for n, (source, target) in enumerate(pairs)]
    for copy in copies:
        copy.start()
    for copy in copies:
        copy.wait()
    rows = q_ref.shape[0]
    slots = k_ref.shape[0]
    facts = [cache_facts(counts_ref, exps_ref, distance, rows) for distance in range(3)]
    for distance, (live, factor, value_scale) in enumerate(facts):
        live_ref[distance : distance + 1, :] = live
        scale_ref[2 * distance : 2 * distance + 1, :] = factor
        scale_ref[2 * distance + 1 : 2 * distance + 2, :] = value_scale
    live, factor, value_scale = facts[0]
    fill_values(v_ref, vt_ref)
    fill_values(nv_ref, nvt_ref)

    def scores(head, slot):
        key = lax.broadcasted_iota(jnp.int32, (rows, rows), 0)
        row = lax.broadcasted_iota(jnp.int32, (rows, rows), 1)
        fresh = jnp.where(key <= row, scores_of(nk_ref[...], q_ref, head), MASKED)
        n_ref[slot] = fresh
        top = fold_max(fresh) * BASE_FACTOR
        for at in range(0, slots, CHUNK):
            cached = cache_scores(k_ref, q_ref, head, at, live)
            s_ref[slot, at : at + CHUNK, :] = cached
            top = jnp.maximum(top, fold_max(cached) * factor)
        return top

    top = scores(0, 0)
    for head in range(GROUP):
        slot = head % 2
        peak = jnp.max(top, axis=0, keepdims=True)
        if head + 1 < GROUP:
            top = scores(head + 1, 1 - slot)
        pn_ref[slot] = jnp.exp2(n_ref[slot] * BASE_FACTOR - peak).astype(jnp.bfloat16)
        for at in range(0, slots, CHUNK):
            p_ref[slot, at : at + CHUNK, :] = jnp.exp2(
                s_ref[slot, at : at + CHUNK, :] * factor - peak
            ).astype(jnp.bfloat16)
        fresh = jnp.dot(nvt_ref[...], pn_ref[slot], preferred_element_type=jnp.float32)
        cached = jnp.dot(vt_ref[...], p_ref[slot], preferred_element_type=jnp.float32)
        acc_ref[head * HD : (head + 1) * HD, :] = fresh[:HD] + value_scale * cached[:HD]
        total_ref[head : head + 1, :] = fresh[HD : HD + 1] + cached[HD : HD + 1]
        peak_ref[head : head + 1, :] = peak


def far_kernel(
    live_ref, scale_ref, q_ref, k_ref, v_ref, acc_in, peak_in, total_in,
    acc_ref, peak_ref, total_ref, vt_ref, s_ref, p_ref, *, distance,
):
    slots = k_ref.shape[0]
    live, factor, value_scale = facts_at(live_ref, scale_ref, distance)
    fill_values(v_ref, vt_ref)

    def scores(head, slot):
        top = None
        for at in range(0, slots, CHUNK):
            cached = cache_scores(k_ref, q_ref, head, at, live)
            s_ref[slot, at : at + CHUNK, :] = cached
            top = fold_max(cached) if top is None else jnp.maximum(top, fold_max(cached))
        return top

    top = scores(0, 0)
    for head in range(GROUP):
        slot = head % 2
        before = peak_in[head : head + 1, :]
        peak = jnp.maximum(before, jnp.max(top, axis=0, keepdims=True) * factor)
        kept = jnp.exp2(before - peak)
        if head + 1 < GROUP:
            top = scores(head + 1, 1 - slot)
        for at in range(0, slots, CHUNK):
            p_ref[slot, at : at + CHUNK, :] = jnp.exp2(
                s_ref[slot, at : at + CHUNK, :] * factor - peak
            ).astype(jnp.bfloat16)
        summed = jnp.dot(vt_ref[...], p_ref[slot], preferred_element_type=jnp.float32)
        at = slice(head * HD, (head + 1) * HD)
        acc_ref[at, :] = acc_in[at, :] * kept + value_scale * summed[:HD]
        total_ref[head : head + 1, :] = total_in[head : head + 1, :] * kept + summed[HD : HD + 1]
        peak_ref[head : head + 1, :] = peak


def last_weights_kernel(live_ref, scale_ref, q_ref, k_ref, peak_in, weights_ref, kept_ref, s_ref, *, distance):
    slots = k_ref.shape[0]
    live, factor, _ = facts_at(live_ref, scale_ref, distance)

    def scores(head, slot):
        top = None
        for at in range(0, slots, CHUNK):
            cached = cache_scores(k_ref, q_ref, head, at, live)
            s_ref[slot, at : at + CHUNK, :] = cached
            top = fold_max(cached) if top is None else jnp.maximum(top, fold_max(cached))
        return top

    top = scores(0, 0)
    for head in range(GROUP):
        slot = head % 2
        before = peak_in[head : head + 1, :]
        peak = jnp.maximum(before, jnp.max(top, axis=0, keepdims=True) * factor)
        kept_ref[head : head + 1, :] = jnp.exp2(before - peak)
        if head + 1 < GROUP:
            top = scores(head + 1, 1 - slot)
        for at in range(0, slots, CHUNK):
            weights_ref[head * slots + at : head * slots + at + CHUNK, :] = jnp.exp2(
                s_ref[slot, at : at + CHUNK, :] * factor - peak
            ).astype(jnp.bfloat16)


def row_plan(head_axis):
    index = lax.axis_index(head_axis)
    chip, core = index // 2, index % 2
    one, three = chip + 1 - 2 * (chip % 2), 3 - chip
    first = jnp.where(core == 0, one, three)
    second = jnp.where(core == 0, three, one)
    opposite = 3 - one
    return chip, core, first, second, opposite


def split_rows(turned_ref, send_ref, keep_ref):
    chip, core, first, second, opposite = row_plan("head")
    block = turned_ref.shape[0] // 8
    for out_ref, owner_core, chips in (
        (send_ref, 1 - core, (chip, first, second, opposite)),
        (keep_ref, core, (chip, second, first, opposite)),
    ):
        for at, owner in enumerate(chips):
            start = pl.multiple_of((2 * owner + owner_core) * block, block)
            out_ref[at * block : (at + 1) * block, :] = turned_ref[pl.ds(start, block), :]


def finish_kernel(
    scale_ref, weights_ref, v_ref, acc_ref, kept_ref, total_ref,
    send_ref, keep_ref, vt_ref, turned_ref, *, distance,
):
    slots = v_ref.shape[0]
    value_scale = scale_ref[2 * distance + 1 : 2 * distance + 2, :]
    fill_values(v_ref, vt_ref)
    for head in range(GROUP):
        summed = jnp.dot(
            vt_ref[...], weights_ref[head * slots : (head + 1) * slots, :],
            preferred_element_type=jnp.float32,
        )
        at = slice(head * HD, (head + 1) * HD)
        kept = kept_ref[head : head + 1, :]
        total = total_ref[head : head + 1, :] * kept + summed[HD : HD + 1]
        attended = (acc_ref[at, :] * kept + value_scale * summed[:HD]) / total
        turned_ref[:, at] = attended.T.astype(jnp.bfloat16)
    split_rows(turned_ref, send_ref, keep_ref)


def project_kernel(keep_ref, got_ref, w_ref, other_w_ref, send_out, keep_out, *, start):
    half, width = keep_out.shape
    step = 512
    for at in range(0, width, step):
        columns = slice(start + at, start + at + step)
        partial = jnp.dot(keep_ref[...], w_ref[:, columns], preferred_element_type=jnp.float32)
        partial += jnp.dot(got_ref[...], other_w_ref[:, columns], preferred_element_type=jnp.float32)
        keep_out[:, at : at + step] = partial[:half]
        send_out[:, at : at + step] = partial[half:].astype(jnp.bfloat16)


def params(mib):
    return pltpu.CompilerParams(vmem_limit_bytes=mib << 20)


def cost(keys, rows, products):
    wide = GROUP * rows * keys
    return pl.CostEstimate(flops=2 * products * wide * HD, transcendentals=wide, bytes_accessed=1 << 20)


def shifted(value, axis, steps):
    count = lax.axis_size(axis)
    return lax.ppermute(value, axis, [(i, i + steps) for i in range(count - steps)])


def core_pairs():
    return [(i, i ^ 1) for i in range(8)]


def chip_pairs(first):
    pairs = []
    for i in range(8):
        chip, core = i // 2, i % 2
        other = chip ^ 1 if (core == 0) == first else chip ^ 3
        pairs.append((i, 2 * other + core))
    return pairs


def on_device(
    queries, new_keys, new_values, cache_keys, cache_values, key_counts, scale_exps, out_weight
):
    rows = queries.shape[0]
    own_keys = cache_keys[0, 0]
    own_values = cache_values[0, 0]
    slots = own_keys.shape[0]
    exps = scale_exps.T
    wide = GROUP * HD
    f32, bf16 = jnp.float32, jnp.bfloat16

    keys_1 = shifted(own_keys, "section", 1)
    values_1 = shifted(own_values, "section", 1)
    other_weight = lax.ppermute(out_weight, "head", core_pairs())
    keys_2 = shifted(keys_1, "section", 1)
    values_2 = shifted(values_1, "section", 1)

    acc_shape = jax.ShapeDtypeStruct((wide, rows), f32)
    row_shape = jax.ShapeDtypeStruct((GROUP, rows), f32)
    vt = lambda n: pltpu.VMEM((HD + ONES_ROWS, n), bf16)
    pair = lambda n, t: pltpu.VMEM((2, n, rows), t)
    acc, peak, total, q, live, scale = pl.pallas_call(
        own_kernel,
        out_shape=(
            acc_shape, row_shape, row_shape, jax.ShapeDtypeStruct(queries.shape, bf16),
            jax.ShapeDtypeStruct((GROUP, rows), jnp.int32), row_shape,
        ),
        in_specs=[HBM] * 7,
        out_specs=(VMEM,) * 6,
        scratch_shapes=[
            pltpu.SMEM(key_counts.shape, jnp.int32), pltpu.SMEM(exps.shape, jnp.int32),
            pltpu.VMEM(new_keys.shape, bf16), pltpu.VMEM(new_values.shape, bf16),
            pltpu.VMEM(own_keys.shape, bf16), pltpu.VMEM(own_values.shape, bf16),
            vt(slots), vt(rows), pair(slots, f32), pair(rows, f32), pair(slots, bf16), pair(rows, bf16),
            pltpu.SemaphoreType.DMA((7,)),
        ],
        compiler_params=params(20),
        cost_estimate=cost(slots + rows, rows, 2),
        name="own",
    )(
        *(
            pltpu.with_memory_space_constraint(value, pltpu.HBM)
            for value in (key_counts, exps, queries, new_keys, new_values, own_keys, own_values)
        )
    )
    acc, peak, total = pl.pallas_call(
        functools.partial(far_kernel, distance=1),
        out_shape=(acc_shape, row_shape, row_shape),
        in_specs=[VMEM] * 8,
        out_specs=(VMEM, VMEM, VMEM),
        scratch_shapes=[vt(slots), pair(slots, f32), pair(slots, bf16)],
        compiler_params=params(16),
        cost_estimate=cost(slots, rows, 2),
        name="far",
    )(live, scale, q, keys_1, values_1, acc, peak, total)
    weights, kept = pl.pallas_call(
        functools.partial(last_weights_kernel, distance=2),
        out_shape=(jax.ShapeDtypeStruct((GROUP * slots, rows), bf16), row_shape),
        in_specs=[VMEM] * 5,
        out_specs=(VMEM, VMEM),
        scratch_shapes=[pair(slots, f32)],
        compiler_params=params(16),
        cost_estimate=cost(slots, rows, 1),
        name="last",
    )(live, scale, q, keys_2, peak)

    half, quarter, eighth = rows // 2, rows // 4, rows // 8
    send, keep = pl.pallas_call(
        functools.partial(finish_kernel, distance=2),
        out_shape=(jax.ShapeDtypeStruct((half, wide), bf16),) * 2,
        in_specs=[VMEM] * 6,
        out_specs=(VMEM, VMEM),
        scratch_shapes=[vt(slots), pltpu.VMEM((rows, wide), bf16)],
        compiler_params=params(16),
        cost_estimate=cost(slots, rows, 1),
        name="finish",
    )(scale, weights, values_2, acc, kept, total)
    got = lax.ppermute(send, "head", core_pairs())

    part = out_weight.shape[1] // 2
    size = lax.axis_size("section")
    pieces = []
    for start in (0, part):
        send, kept_rows = pl.pallas_call(
            functools.partial(project_kernel, start=start),
            out_shape=(jax.ShapeDtypeStruct((quarter, part), bf16), jax.ShapeDtypeStruct((quarter, part), f32)),
            in_specs=[VMEM] * 4,
            out_specs=(VMEM, VMEM),
            compiler_params=params(16),
            cost_estimate=pl.CostEstimate(
                flops=2 * rows * wide * part, transcendentals=0, bytes_accessed=1 << 20
            ),
            name="project",
        )(keep, got, out_weight, other_weight)
        first = lax.ppermute(send, "head", chip_pairs(True))
        two = kept_rows + first.astype(f32)
        second = lax.ppermute(two[eighth:].astype(bf16), "head", chip_pairs(False))
        done = (two[:eighth] + second.astype(f32)).astype(bf16)
        pieces.append(lax.ppermute(done, "section", [(i, (i + 1) % size) for i in range(size)]))
    return jnp.concatenate(pieces, axis=1).astype(f32)


def solution(mesh):
    in_specs = (
        P("section", "head"),
        P("section", "head"),
        P("section", "head"),
        P("section", "head", None, None),
        P("section", "head", None, None),
        P(),
        P(),
        P("head", None),
    )
    out_specs = P(("section", "head"), None)
    return jax.shard_map(on_device, mesh=mesh, in_specs=in_specs, out_specs=out_specs, check_vma=False)
```

```python
import functools
import math

import jax
import jax.numpy as jnp
from jax import lax
from jax.experimental import pallas as pl
from jax.experimental.pallas import tpu as pltpu
from jax.sharding import PartitionSpec as P


HD = 128
GROUP = 8
MASKED = -1e30
LOG2E = 1.4426950408889634
BASE_FACTOR = LOG2E / math.sqrt(HD)
CHUNK = 256
ONES_ROWS = 16

VMEM = pl.BlockSpec(memory_space=pltpu.VMEM)
HBM = pl.BlockSpec(memory_space=pltpu.HBM)


def cache_facts(counts_ref, exps_ref, distance, width):
    index = lax.axis_index("section") - distance
    source = jnp.maximum(index, 0)
    live = jnp.full((1, width), jnp.where(index >= 0, counts_ref[source], 0), jnp.int32)
    key_exp = jnp.full((1, width), exps_ref[0, source], jnp.int32).astype(jnp.float32)
    value_exp = jnp.full((1, width), exps_ref[1, source], jnp.int32).astype(jnp.float32)
    factor = jnp.where(live > 0, jnp.exp2(key_exp), 1.0) * BASE_FACTOR
    return live, factor, jnp.exp2(value_exp)


def facts_at(live_ref, scale_ref, distance):
    return (
        live_ref[distance : distance + 1, :],
        scale_ref[2 * distance : 2 * distance + 1, :],
        scale_ref[2 * distance + 1 : 2 * distance + 2, :],
    )


def fold_max(block):
    top = block[0:8]
    for at in range(8, block.shape[0], 8):
        top = jnp.maximum(top, block[at : at + 8])
    return top


def scores_of(key_block, q_ref, head):
    q = q_ref[:, head * HD : (head + 1) * HD]
    return lax.dot_general(key_block, q, (((1,), (1,)), ((), ())), preferred_element_type=jnp.float32)


def cache_scores(keys_ref, q_ref, head, at):
    return scores_of(keys_ref[at : at + CHUNK, :], q_ref, head)


def fill_keys(k_ref, spare_ref, live, keys_ref):
    keys = k_ref[...].astype(jnp.float32)
    spare = jnp.where(live[:, :HD] > 0, keys[0:1], spare_ref[0:1, :].astype(jnp.float32))
    slot = lax.broadcasted_iota(jnp.int32, keys.shape, 0)
    keys_ref[...] = jnp.where(slot < live[:, :HD], keys, spare).astype(jnp.bfloat16)


def fill_values(v_ref, vt_ref, live=None):
    slots = v_ref.shape[0]
    values = v_ref[...]
    ones = jnp.ones((ONES_ROWS, slots), jnp.float32)
    if live is not None:
        slot = lax.broadcasted_iota(jnp.int32, values.shape, 0)
        values = jnp.where(slot < live[:, :HD], values.astype(jnp.float32), 0.0).astype(jnp.bfloat16)
        lane = lax.broadcasted_iota(jnp.int32, ones.shape, 1)
        ones = jnp.where(lane < jnp.concatenate([live[:, :HD]] * (slots // HD), axis=1), ones, 0.0)
    vt_ref[:HD, :] = values.T
    vt_ref[HD:, :] = ones.astype(jnp.bfloat16)


def near_kernel(
    counts_hbm, exps_hbm, q_hbm, nk_hbm, nv_hbm, k_hbm, v_hbm, far_k_ref, far_v_ref,
    acc_ref, peak_ref, total_ref, q_ref, live_ref, scale_ref, nk_ref,
    counts_ref, exps_ref, nv_ref, k_ref, v_ref, keys_ref, far_keys_ref,
    vt_ref, far_vt_ref, nvt_ref, s_ref, far_s_ref, n_ref, p_ref, far_p_ref, pn_ref, sems,
):
    pairs = (
        (q_hbm, q_ref), (counts_hbm, counts_ref), (exps_hbm, exps_ref), (nk_hbm, nk_ref),
        (k_hbm, k_ref), (nv_hbm, nv_ref), (v_hbm, v_ref),
    )
    copies = [pltpu.make_async_copy(source, target, sems.at[n]) for n, (source, target) in enumerate(pairs)]
    for copy in copies:
        copy.start()
    for copy in copies:
        copy.wait()
    rows = q_ref.shape[0]
    slots = k_ref.shape[0]
    facts = [cache_facts(counts_ref, exps_ref, distance, rows) for distance in range(3)]
    for distance, (live, factor, value_scale) in enumerate(facts):
        live_ref[distance : distance + 1, :] = live
        scale_ref[2 * distance : 2 * distance + 1, :] = factor
        scale_ref[2 * distance + 1 : 2 * distance + 2, :] = value_scale
    fill_keys(k_ref, nk_ref, facts[0][0], keys_ref)
    fill_keys(far_k_ref, nk_ref, facts[1][0], far_keys_ref)
    fill_values(nv_ref, nvt_ref)
    fill_values(v_ref, vt_ref, facts[0][0])
    fill_values(far_v_ref, far_vt_ref, facts[1][0])
    caches = (
        (keys_ref, vt_ref, s_ref, p_ref) + facts[0][1:],
        (far_keys_ref, far_vt_ref, far_s_ref, far_p_ref) + facts[1][1:],
    )

    def scores(head, slot):
        key = lax.broadcasted_iota(jnp.int32, (rows, rows), 0)
        row = lax.broadcasted_iota(jnp.int32, (rows, rows), 1)
        fresh = jnp.where(key <= row, scores_of(nk_ref[...], q_ref, head), MASKED)
        n_ref[slot] = fresh
        top = fold_max(fresh) * BASE_FACTOR
        for keys, _, kept_scores, _, factor, _ in caches:
            for at in range(0, slots, CHUNK):
                cached = cache_scores(keys, q_ref, head, at)
                kept_scores[slot, at : at + CHUNK, :] = cached
                top = jnp.maximum(top, fold_max(cached) * factor)
        return top

    top = scores(0, 0)
    for head in range(GROUP):
        slot = head % 2
        peak = jnp.max(top, axis=0, keepdims=True)
        if head + 1 < GROUP:
            top = scores(head + 1, 1 - slot)
        pn_ref[slot] = jnp.exp2(n_ref[slot] * BASE_FACTOR - peak).astype(jnp.bfloat16)
        summed = jnp.dot(nvt_ref[...], pn_ref[slot], preferred_element_type=jnp.float32)
        acc, total = summed[:HD], summed[HD : HD + 1]
        for _, values, kept_scores, weights, factor, value_scale in caches:
            for at in range(0, slots, CHUNK):
                weights[slot, at : at + CHUNK, :] = jnp.exp2(
                    kept_scores[slot, at : at + CHUNK, :] * factor - peak
                ).astype(jnp.bfloat16)
            summed = jnp.dot(values[...], weights[slot], preferred_element_type=jnp.float32)
            acc += value_scale * summed[:HD]
            total += summed[HD : HD + 1]
        acc_ref[head * HD : (head + 1) * HD, :] = acc
        total_ref[head : head + 1, :] = total
        peak_ref[head : head + 1, :] = peak


def last_weights_kernel(
    live_ref, scale_ref, q_ref, nk_ref, k_ref, peak_in, weights_ref, kept_ref, s_ref, keys_ref, *, distance
):
    slots = k_ref.shape[0]
    live, factor, _ = facts_at(live_ref, scale_ref, distance)
    fill_keys(k_ref, nk_ref, live, keys_ref)

    def scores(head, slot):
        top = None
        for at in range(0, slots, CHUNK):
            cached = cache_scores(keys_ref, q_ref, head, at)
            s_ref[slot, at : at + CHUNK, :] = cached
            top = fold_max(cached) if top is None else jnp.maximum(top, fold_max(cached))
        return top

    top = scores(0, 0)
    for head in range(GROUP):
        slot = head % 2
        before = peak_in[head : head + 1, :]
        peak = jnp.maximum(before, jnp.max(top, axis=0, keepdims=True) * factor)
        kept_ref[head : head + 1, :] = jnp.exp2(before - peak)
        if head + 1 < GROUP:
            top = scores(head + 1, 1 - slot)
        for at in range(0, slots, CHUNK):
            weights_ref[head * slots + at : head * slots + at + CHUNK, :] = jnp.exp2(
                s_ref[slot, at : at + CHUNK, :] * factor - peak
            ).astype(jnp.bfloat16)


def row_plan(head_axis):
    index = lax.axis_index(head_axis)
    chip, core = index // 2, index % 2
    one, three = chip + 1 - 2 * (chip % 2), 3 - chip
    first = jnp.where(core == 0, one, three)
    second = jnp.where(core == 0, three, one)
    opposite = 3 - one
    return chip, core, first, second, opposite


def split_rows(turned_ref, send_ref, keep_ref):
    chip, core, first, second, opposite = row_plan("head")
    block = turned_ref.shape[0] // 8
    for out_ref, owner_core, chips in (
        (send_ref, 1 - core, (chip, first, second, opposite)),
        (keep_ref, core, (chip, second, first, opposite)),
    ):
        for at, owner in enumerate(chips):
            start = pl.multiple_of((2 * owner + owner_core) * block, block)
            out_ref[at * block : (at + 1) * block, :] = turned_ref[pl.ds(start, block), :]


def finish_kernel(
    live_ref, scale_ref, weights_ref, v_ref, acc_ref, kept_ref, total_ref,
    send_ref, keep_ref, vt_ref, turned_ref, *, distance,
):
    slots = v_ref.shape[0]
    live, _, value_scale = facts_at(live_ref, scale_ref, distance)
    fill_values(v_ref, vt_ref, live)
    for head in range(GROUP):
        summed = jnp.dot(
            vt_ref[...], weights_ref[head * slots : (head + 1) * slots, :],
            preferred_element_type=jnp.float32,
        )
        at = slice(head * HD, (head + 1) * HD)
        kept = kept_ref[head : head + 1, :]
        total = total_ref[head : head + 1, :] * kept + summed[HD : HD + 1]
        attended = (acc_ref[at, :] * kept + value_scale * summed[:HD]) / total
        turned_ref[:, at] = attended.T.astype(jnp.bfloat16)
    split_rows(turned_ref, send_ref, keep_ref)


def project_own_kernel(keep_ref, w_ref, out_ref):
    step = 512
    for at in range(0, out_ref.shape[1], step):
        columns = slice(at, at + step)
        out_ref[:, columns] = jnp.dot(keep_ref[...], w_ref[:, columns], preferred_element_type=jnp.float32)


def project_kernel(own_ref, got_ref, other_w_ref, send_out, keep_out, *, start):
    half, width = keep_out.shape
    step = 512
    for at in range(0, width, step):
        columns = slice(start + at, start + at + step)
        partial = own_ref[:, columns] + jnp.dot(
            got_ref[...], other_w_ref[:, columns], preferred_element_type=jnp.float32
        )
        keep_out[:, at : at + step] = partial[:half]
        send_out[:, at : at + step] = partial[half:].astype(jnp.bfloat16)


def params(mib):
    return pltpu.CompilerParams(vmem_limit_bytes=mib << 20)


def cost(keys, rows, products):
    wide = GROUP * rows * keys
    return pl.CostEstimate(flops=2 * products * wide * HD, transcendentals=wide, bytes_accessed=1 << 20)


def shifted(value, axis, steps):
    count = lax.axis_size(axis)
    return lax.ppermute(value, axis, [(i, i + steps) for i in range(count - steps)])


def core_pairs():
    return [(i, i ^ 1) for i in range(8)]


def chip_pairs(first):
    pairs = []
    for i in range(8):
        chip, core = i // 2, i % 2
        other = chip ^ 1 if (core == 0) == first else chip ^ 3
        pairs.append((i, 2 * other + core))
    return pairs


def on_device(
    queries, new_keys, new_values, cache_keys, cache_values, key_counts, scale_exps, out_weight
):
    rows = queries.shape[0]
    own_keys = cache_keys[0, 0]
    own_values = cache_values[0, 0]
    slots = own_keys.shape[0]
    exps = scale_exps.T
    wide = GROUP * HD
    f32, bf16 = jnp.float32, jnp.bfloat16

    keys_1 = shifted(own_keys, "section", 1)
    values_1 = shifted(own_values, "section", 1)
    other_weight = lax.ppermute(out_weight, "head", core_pairs())
    keys_2 = shifted(keys_1, "section", 1)
    values_2 = shifted(values_1, "section", 1)

    acc_shape = jax.ShapeDtypeStruct((wide, rows), f32)
    row_shape = jax.ShapeDtypeStruct((GROUP, rows), f32)
    vt = lambda n: pltpu.VMEM((HD + ONES_ROWS, n), bf16)
    pair = lambda n, t: pltpu.VMEM((2, n, rows), t)
    local = (key_counts, exps, queries, new_keys, new_values, own_keys, own_values)
    acc, peak, total, q, live, scale, near_keys = pl.pallas_call(
        near_kernel,
        out_shape=(
            acc_shape, row_shape, row_shape, jax.ShapeDtypeStruct(queries.shape, bf16),
            jax.ShapeDtypeStruct((GROUP, rows), jnp.int32), row_shape,
            jax.ShapeDtypeStruct(new_keys.shape, bf16),
        ),
        in_specs=[HBM] * 7 + [VMEM] * 2,
        out_specs=(VMEM,) * 7,
        scratch_shapes=[
            pltpu.SMEM(key_counts.shape, jnp.int32), pltpu.SMEM(exps.shape, jnp.int32),
            pltpu.VMEM(new_values.shape, bf16),
            pltpu.VMEM(own_keys.shape, bf16), pltpu.VMEM(own_values.shape, bf16),
            pltpu.VMEM(own_keys.shape, bf16), pltpu.VMEM(own_keys.shape, bf16),
            vt(slots), vt(slots), vt(rows),
            pair(slots, f32), pair(slots, f32), pair(rows, f32),
            pair(slots, bf16), pair(slots, bf16), pair(rows, bf16),
            pltpu.SemaphoreType.DMA((7,)),
        ],
        compiler_params=params(24),
        cost_estimate=cost(2 * slots + rows, rows, 2),
        name="near",
    )(*(pltpu.with_memory_space_constraint(value, pltpu.HBM) for value in local), keys_1, values_1)
    weights, kept = pl.pallas_call(
        functools.partial(last_weights_kernel, distance=2),
        out_shape=(jax.ShapeDtypeStruct((GROUP * slots, rows), bf16), row_shape),
        in_specs=[VMEM] * 6,
        out_specs=(VMEM, VMEM),
        scratch_shapes=[pair(slots, f32), pltpu.VMEM(own_keys.shape, bf16)],
        compiler_params=params(16),
        cost_estimate=cost(slots, rows, 1),
        name="last",
    )(live, scale, q, near_keys, keys_2, peak)

    half, quarter, eighth = rows // 2, rows // 4, rows // 8
    send, keep = pl.pallas_call(
        functools.partial(finish_kernel, distance=2),
        out_shape=(jax.ShapeDtypeStruct((half, wide), bf16),) * 2,
        in_specs=[VMEM] * 7,
        out_specs=(VMEM, VMEM),
        scratch_shapes=[vt(slots), pltpu.VMEM((rows, wide), bf16)],
        compiler_params=params(16),
        cost_estimate=cost(slots, rows, 1),
        name="finish",
    )(live, scale, weights, values_2, acc, kept, total)
    got = lax.ppermute(send, "head", core_pairs())
    own_share = pl.pallas_call(
        project_own_kernel,
        out_shape=jax.ShapeDtypeStruct((half, out_weight.shape[1]), f32),
        in_specs=[VMEM] * 2,
        out_specs=VMEM,
        compiler_params=params(16),
        cost_estimate=pl.CostEstimate(
            flops=2 * half * wide * out_weight.shape[1], transcendentals=0, bytes_accessed=1 << 20
        ),
        name="project_own",
    )(keep, out_weight)

    part = out_weight.shape[1] // 2
    size = lax.axis_size("section")
    pieces = []
    for start in (0, part):
        send, kept_rows = pl.pallas_call(
            functools.partial(project_kernel, start=start),
            out_shape=(jax.ShapeDtypeStruct((quarter, part), bf16), jax.ShapeDtypeStruct((quarter, part), f32)),
            in_specs=[VMEM] * 3,
            out_specs=(VMEM, VMEM),
            compiler_params=params(16),
            cost_estimate=pl.CostEstimate(
                flops=rows * wide * part, transcendentals=0, bytes_accessed=1 << 20
            ),
            name="project",
        )(own_share, got, other_weight)
        first = lax.ppermute(send, "head", chip_pairs(True))
        two = kept_rows + first.astype(f32)
        second = lax.ppermute(two[eighth:].astype(bf16), "head", chip_pairs(False))
        done = (two[:eighth] + second.astype(f32)).astype(bf16)
        pieces.append(lax.ppermute(done, "section", [(i, (i + 1) % size) for i in range(size)]))
    return jnp.concatenate(pieces, axis=1).astype(f32)


def solution(mesh):
    in_specs = (
        P("section", "head"),
        P("section", "head"),
        P("section", "head"),
        P("section", "head", None, None),
        P("section", "head", None, None),
        P(),
        P(),
        P("head", None),
    )
    out_specs = P(("section", "head"), None)
    return jax.shard_map(on_device, mesh=mesh, in_specs=in_specs, out_specs=out_specs, check_vma=False)
```

```python
import functools
import math

import jax
import jax.numpy as jnp
from jax import lax
from jax.experimental import pallas as pl
from jax.experimental.pallas import tpu as pltpu
from jax.sharding import PartitionSpec as P


HD = 128
GROUP = 8
MASKED = -1e30
LOG2E = 1.4426950408889634
BASE_FACTOR = LOG2E / math.sqrt(HD)
CHUNK = 256
ONES_ROWS = 16

VMEM = pl.BlockSpec(memory_space=pltpu.VMEM)
HBM = pl.BlockSpec(memory_space=pltpu.HBM)


def cache_facts(counts_ref, exps_ref, distance, width):
    index = lax.axis_index("section") - distance
    source = jnp.maximum(index, 0)
    live = jnp.full((1, width), jnp.where(index >= 0, counts_ref[source], 0), jnp.int32)
    key_exp = jnp.full((1, width), exps_ref[0, source], jnp.int32).astype(jnp.float32)
    value_exp = jnp.full((1, width), exps_ref[1, source], jnp.int32).astype(jnp.float32)
    factor = jnp.where(live > 0, jnp.exp2(key_exp), 1.0) * BASE_FACTOR
    return live, factor, jnp.exp2(value_exp)


def facts_at(live_ref, scale_ref, distance):
    return (
        live_ref[distance : distance + 1, :],
        scale_ref[2 * distance : 2 * distance + 1, :],
        scale_ref[2 * distance + 1 : 2 * distance + 2, :],
    )


def fold_max(block):
    top = block[0:8]
    for at in range(8, block.shape[0], 8):
        top = jnp.maximum(top, block[at : at + 8])
    return top


def scores_of(key_block, q_ref, head):
    q = q_ref[:, head * HD : (head + 1) * HD]
    return lax.dot_general(key_block, q, (((1,), (1,)), ((), ())), preferred_element_type=jnp.float32)


def cache_scores(keys_ref, q_ref, head, at):
    return scores_of(keys_ref[at : at + CHUNK, :], q_ref, head)


def fill_keys(k_ref, spare_ref, live, keys_ref):
    keys = k_ref[...].astype(jnp.float32)
    spare = jnp.where(live[:, :HD] > 0, keys[0:1], spare_ref[0:1, :].astype(jnp.float32))
    slot = lax.broadcasted_iota(jnp.int32, keys.shape, 0)
    keys_ref[...] = jnp.where(slot < live[:, :HD], keys, spare).astype(jnp.bfloat16)


def fill_values(v_ref, vt_ref, live=None):
    slots = v_ref.shape[0]
    values = v_ref[...]
    ones = jnp.ones((ONES_ROWS, slots), jnp.float32)
    if live is not None:
        slot = lax.broadcasted_iota(jnp.int32, values.shape, 0)
        values = jnp.where(slot < live[:, :HD], values.astype(jnp.float32), 0.0).astype(jnp.bfloat16)
        lane = lax.broadcasted_iota(jnp.int32, ones.shape, 1)
        ones = jnp.where(lane < jnp.concatenate([live[:, :HD]] * (slots // HD), axis=1), ones, 0.0)
    vt_ref[:HD, :] = values.T
    vt_ref[HD:, :] = ones.astype(jnp.bfloat16)


def prepare_kernel(
    counts_hbm, exps_hbm, q_hbm, nk_hbm, nv_hbm, k_hbm, v_hbm,
    q_ref, live_ref, scale_ref, nk_ref, keys_ref, vt_ref, nvt_ref,
    counts_ref, exps_ref, nv_ref, k_ref, v_ref, sems,
):
    pairs = (
        (counts_hbm, counts_ref), (exps_hbm, exps_ref), (nk_hbm, nk_ref), (k_hbm, k_ref),
        (nv_hbm, nv_ref), (v_hbm, v_ref), (q_hbm, q_ref),
    )
    copies = [pltpu.make_async_copy(source, target, sems.at[n]) for n, (source, target) in enumerate(pairs)]
    for copy in copies:
        copy.start()
    for copy in copies:
        copy.wait()
    facts = [cache_facts(counts_ref, exps_ref, distance, q_ref.shape[0]) for distance in range(3)]
    for distance, (live, factor, value_scale) in enumerate(facts):
        live_ref[distance : distance + 1, :] = live
        scale_ref[2 * distance : 2 * distance + 1, :] = factor
        scale_ref[2 * distance + 1 : 2 * distance + 2, :] = value_scale
    fill_keys(k_ref, nk_ref, facts[0][0], keys_ref)
    fill_values(nv_ref, nvt_ref)
    fill_values(v_ref, vt_ref, facts[0][0])


def near_kernel(
    q_ref, live_ref, scale_ref, nk_ref, keys_ref, vt_ref, nvt_ref, far_k_ref, far_v_ref,
    acc_ref, peak_ref, total_ref,
    far_keys_ref, far_vt_ref, s_ref, far_s_ref, n_ref, p_ref, far_p_ref, pn_ref,
):
    rows = q_ref.shape[0]
    slots = far_k_ref.shape[0]
    facts = [facts_at(live_ref, scale_ref, distance) for distance in range(2)]
    fill_keys(far_k_ref, nk_ref, facts[1][0], far_keys_ref)
    fill_values(far_v_ref, far_vt_ref, facts[1][0])
    caches = (
        (keys_ref, vt_ref, s_ref, p_ref) + facts[0][1:],
        (far_keys_ref, far_vt_ref, far_s_ref, far_p_ref) + facts[1][1:],
    )

    def scores(head, slot):
        key = lax.broadcasted_iota(jnp.int32, (rows, rows), 0)
        row = lax.broadcasted_iota(jnp.int32, (rows, rows), 1)
        fresh = jnp.where(key <= row, scores_of(nk_ref[...], q_ref, head), MASKED)
        n_ref[slot] = fresh
        top = fold_max(fresh) * BASE_FACTOR
        for keys, _, kept_scores, _, factor, _ in caches:
            for at in range(0, slots, CHUNK):
                cached = cache_scores(keys, q_ref, head, at)
                kept_scores[slot, at : at + CHUNK, :] = cached
                top = jnp.maximum(top, fold_max(cached) * factor)
        return top

    top = scores(0, 0)
    for head in range(GROUP):
        slot = head % 2
        peak = jnp.max(top, axis=0, keepdims=True)
        if head + 1 < GROUP:
            top = scores(head + 1, 1 - slot)
        pn_ref[slot] = jnp.exp2(n_ref[slot] * BASE_FACTOR - peak).astype(jnp.bfloat16)
        summed = jnp.dot(nvt_ref[...], pn_ref[slot], preferred_element_type=jnp.float32)
        acc, total = summed[:HD], summed[HD : HD + 1]
        for _, values, kept_scores, weights, factor, value_scale in caches:
            for at in range(0, slots, CHUNK):
                weights[slot, at : at + CHUNK, :] = jnp.exp2(
                    kept_scores[slot, at : at + CHUNK, :] * factor - peak
                ).astype(jnp.bfloat16)
            summed = jnp.dot(values[...], weights[slot], preferred_element_type=jnp.float32)
            acc += value_scale * summed[:HD]
            total += summed[HD : HD + 1]
        acc_ref[head * HD : (head + 1) * HD, :] = acc
        total_ref[head : head + 1, :] = total
        peak_ref[head : head + 1, :] = peak


def last_weights_kernel(
    live_ref, scale_ref, q_ref, nk_ref, k_ref, peak_in, weights_ref, kept_ref, s_ref, keys_ref, *, distance
):
    slots = k_ref.shape[0]
    live, factor, _ = facts_at(live_ref, scale_ref, distance)
    fill_keys(k_ref, nk_ref, live, keys_ref)

    def scores(head, slot):
        top = None
        for at in range(0, slots, CHUNK):
            cached = cache_scores(keys_ref, q_ref, head, at)
            s_ref[slot, at : at + CHUNK, :] = cached
            top = fold_max(cached) if top is None else jnp.maximum(top, fold_max(cached))
        return top

    top = scores(0, 0)
    for head in range(GROUP):
        slot = head % 2
        before = peak_in[head : head + 1, :]
        peak = jnp.maximum(before, jnp.max(top, axis=0, keepdims=True) * factor)
        kept_ref[head : head + 1, :] = jnp.exp2(before - peak)
        if head + 1 < GROUP:
            top = scores(head + 1, 1 - slot)
        for at in range(0, slots, CHUNK):
            weights_ref[head * slots + at : head * slots + at + CHUNK, :] = jnp.exp2(
                s_ref[slot, at : at + CHUNK, :] * factor - peak
            ).astype(jnp.bfloat16)


def row_plan(head_axis):
    index = lax.axis_index(head_axis)
    chip, core = index // 2, index % 2
    one, three = chip + 1 - 2 * (chip % 2), 3 - chip
    first = jnp.where(core == 0, one, three)
    second = jnp.where(core == 0, three, one)
    opposite = 3 - one
    return chip, core, first, second, opposite


def split_rows(turned_ref, send_ref, keep_ref):
    chip, core, first, second, opposite = row_plan("head")
    block = turned_ref.shape[0] // 8
    for out_ref, owner_core, chips in (
        (send_ref, 1 - core, (chip, first, second, opposite)),
        (keep_ref, core, (chip, second, first, opposite)),
    ):
        for at, owner in enumerate(chips):
            start = pl.multiple_of((2 * owner + owner_core) * block, block)
            out_ref[at * block : (at + 1) * block, :] = turned_ref[pl.ds(start, block), :]


def finish_kernel(
    live_ref, scale_ref, weights_ref, v_ref, acc_ref, kept_ref, total_ref,
    send_ref, keep_ref, vt_ref, turned_ref, *, distance,
):
    slots = v_ref.shape[0]
    live, _, value_scale = facts_at(live_ref, scale_ref, distance)
    fill_values(v_ref, vt_ref, live)
    for head in range(GROUP):
        summed = jnp.dot(
            vt_ref[...], weights_ref[head * slots : (head + 1) * slots, :],
            preferred_element_type=jnp.float32,
        )
        at = slice(head * HD, (head + 1) * HD)
        kept = kept_ref[head : head + 1, :]
        total = total_ref[head : head + 1, :] * kept + summed[HD : HD + 1]
        attended = (acc_ref[at, :] * kept + value_scale * summed[:HD]) / total
        turned_ref[:, at] = attended.T.astype(jnp.bfloat16)
    split_rows(turned_ref, send_ref, keep_ref)


def project_own_kernel(keep_ref, w_ref, out_ref):
    step = 512
    for at in range(0, out_ref.shape[1], step):
        columns = slice(at, at + step)
        out_ref[:, columns] = jnp.dot(keep_ref[...], w_ref[:, columns], preferred_element_type=jnp.float32)


def project_kernel(own_ref, got_ref, other_w_ref, send_out, keep_out, *, start):
    half, width = keep_out.shape
    step = 512
    for at in range(0, width, step):
        columns = slice(start + at, start + at + step)
        partial = own_ref[:, columns] + jnp.dot(
            got_ref[...], other_w_ref[:, columns], preferred_element_type=jnp.float32
        )
        keep_out[:, at : at + step] = partial[:half]
        send_out[:, at : at + step] = partial[half:].astype(jnp.bfloat16)


def params(mib):
    return pltpu.CompilerParams(vmem_limit_bytes=mib << 20)


def cost(keys, rows, products):
    wide = GROUP * rows * keys
    return pl.CostEstimate(flops=2 * products * wide * HD, transcendentals=wide, bytes_accessed=1 << 20)


def shifted(value, axis, steps):
    count = lax.axis_size(axis)
    return lax.ppermute(value, axis, [(i, i + steps) for i in range(count - steps)])


def core_pairs():
    return [(i, i ^ 1) for i in range(8)]


def chip_pairs(first):
    pairs = []
    for i in range(8):
        chip, core = i // 2, i % 2
        other = chip ^ 1 if (core == 0) == first else chip ^ 3
        pairs.append((i, 2 * other + core))
    return pairs


def on_device(
    queries, new_keys, new_values, cache_keys, cache_values, key_counts, scale_exps, out_weight
):
    rows = queries.shape[0]
    own_keys = cache_keys[0, 0]
    own_values = cache_values[0, 0]
    slots = own_keys.shape[0]
    exps = scale_exps.T
    wide = GROUP * HD
    f32, bf16 = jnp.float32, jnp.bfloat16

    keys_1 = shifted(own_keys, "section", 1)
    values_1 = shifted(own_values, "section", 1)
    other_weight = lax.ppermute(out_weight, "head", core_pairs())
    keys_2 = shifted(keys_1, "section", 1)
    values_2 = shifted(values_1, "section", 1)

    acc_shape = jax.ShapeDtypeStruct((wide, rows), f32)
    row_shape = jax.ShapeDtypeStruct((GROUP, rows), f32)
    vt = lambda n: pltpu.VMEM((HD + ONES_ROWS, n), bf16)
    pair = lambda n, t: pltpu.VMEM((2, n, rows), t)
    local = (key_counts, exps, queries, new_keys, new_values, own_keys, own_values)
    like = lambda *shape: jax.ShapeDtypeStruct(shape, bf16)
    ready = pl.pallas_call(
        prepare_kernel,
        out_shape=(
            like(*queries.shape), jax.ShapeDtypeStruct((GROUP, rows), jnp.int32), row_shape,
            like(*new_keys.shape), like(*own_keys.shape), like(HD + ONES_ROWS, slots), like(HD + ONES_ROWS, rows),
        ),
        in_specs=[HBM] * 7,
        out_specs=(VMEM,) * 7,
        scratch_shapes=[
            pltpu.SMEM(key_counts.shape, jnp.int32), pltpu.SMEM(exps.shape, jnp.int32),
            pltpu.VMEM(new_values.shape, bf16), pltpu.VMEM(own_keys.shape, bf16),
            pltpu.VMEM(own_values.shape, bf16), pltpu.SemaphoreType.DMA((7,)),
        ],
        compiler_params=params(8),
        cost_estimate=pl.CostEstimate(flops=1 << 20, transcendentals=0, bytes_accessed=1 << 20),
        name="prepare",
    )(*(pltpu.with_memory_space_constraint(value, pltpu.HBM) for value in local))
    q, live, scale, near_keys = ready[:4]
    acc, peak, total = pl.pallas_call(
        near_kernel,
        out_shape=(acc_shape, row_shape, row_shape),
        in_specs=[VMEM] * 9,
        out_specs=(VMEM,) * 3,
        scratch_shapes=[
            pltpu.VMEM(own_keys.shape, bf16), vt(slots),
            pair(slots, f32), pair(slots, f32), pair(rows, f32),
            pair(slots, bf16), pair(slots, bf16), pair(rows, bf16),
        ],
        compiler_params=params(24),
        cost_estimate=cost(2 * slots + rows, rows, 2),
        name="near",
    )(*ready, keys_1, values_1)
    weights, kept = pl.pallas_call(
        functools.partial(last_weights_kernel, distance=2),
        out_shape=(jax.ShapeDtypeStruct((GROUP * slots, rows), bf16), row_shape),
        in_specs=[VMEM] * 6,
        out_specs=(VMEM, VMEM),
        scratch_shapes=[pair(slots, f32), pltpu.VMEM(own_keys.shape, bf16)],
        compiler_params=params(16),
        cost_estimate=cost(slots, rows, 1),
        name="last",
    )(live, scale, q, near_keys, keys_2, peak)

    half, quarter, eighth = rows // 2, rows // 4, rows // 8
    send, keep = pl.pallas_call(
        functools.partial(finish_kernel, distance=2),
        out_shape=(jax.ShapeDtypeStruct((half, wide), bf16),) * 2,
        in_specs=[VMEM] * 7,
        out_specs=(VMEM, VMEM),
        scratch_shapes=[vt(slots), pltpu.VMEM((rows, wide), bf16)],
        compiler_params=params(16),
        cost_estimate=cost(slots, rows, 1),
        name="finish",
    )(live, scale, weights, values_2, acc, kept, total)
    got = lax.ppermute(send, "head", core_pairs())
    own_share = pl.pallas_call(
        project_own_kernel,
        out_shape=jax.ShapeDtypeStruct((half, out_weight.shape[1]), f32),
        in_specs=[VMEM] * 2,
        out_specs=VMEM,
        compiler_params=params(16),
        cost_estimate=pl.CostEstimate(
            flops=2 * half * wide * out_weight.shape[1], transcendentals=0, bytes_accessed=1 << 20
        ),
        name="project_own",
    )(keep, out_weight)

    part = out_weight.shape[1] // 2
    size = lax.axis_size("section")
    pieces = []
    for start in (0, part):
        send, kept_rows = pl.pallas_call(
            functools.partial(project_kernel, start=start),
            out_shape=(jax.ShapeDtypeStruct((quarter, part), bf16), jax.ShapeDtypeStruct((quarter, part), f32)),
            in_specs=[VMEM] * 3,
            out_specs=(VMEM, VMEM),
            compiler_params=params(16),
            cost_estimate=pl.CostEstimate(
                flops=rows * wide * part, transcendentals=0, bytes_accessed=1 << 20
            ),
            name="project",
        )(own_share, got, other_weight)
        first = lax.ppermute(send, "head", chip_pairs(True))
        two = kept_rows + first.astype(f32)
        second = lax.ppermute(two[eighth:].astype(bf16), "head", chip_pairs(False))
        done = (two[:eighth] + second.astype(f32)).astype(bf16)
        pieces.append(lax.ppermute(done, "section", [(i, (i + 1) % size) for i in range(size)]))
    return jnp.concatenate(pieces, axis=1).astype(f32)


def solution(mesh):
    in_specs = (
        P("section", "head"),
        P("section", "head"),
        P("section", "head"),
        P("section", "head", None, None),
        P("section", "head", None, None),
        P(),
        P(),
        P("head", None),
    )
    out_specs = P(("section", "head"), None)
    return jax.shard_map(on_device, mesh=mesh, in_specs=in_specs, out_specs=out_specs, check_vma=False)
```

```python
import functools
import math

import jax
import jax.numpy as jnp
from jax import lax
from jax.experimental import pallas as pl
from jax.experimental.pallas import tpu as pltpu
from jax.sharding import PartitionSpec as P


HD = 128
GROUP = 8
MASKED = -1e30
LOG2E = 1.4426950408889634
BASE_FACTOR = LOG2E / math.sqrt(HD)
CHUNK = 256
ONES_ROWS = 16

VMEM = pl.BlockSpec(memory_space=pltpu.VMEM)
HBM = pl.BlockSpec(memory_space=pltpu.HBM)


def cache_facts(counts_ref, exps_ref, distance, width):
    index = lax.axis_index("section") - distance
    source = jnp.maximum(index, 0)
    live = jnp.full((1, width), jnp.where(index >= 0, counts_ref[source], 0), jnp.int32)
    key_exp = jnp.full((1, width), exps_ref[0, source], jnp.int32).astype(jnp.float32)
    value_exp = jnp.full((1, width), exps_ref[1, source], jnp.int32).astype(jnp.float32)
    factor = jnp.where(live > 0, jnp.exp2(key_exp), 1.0) * BASE_FACTOR
    return live, factor, jnp.exp2(value_exp)


def facts_at(live_ref, scale_ref, distance):
    return (
        live_ref[distance : distance + 1, :],
        scale_ref[2 * distance : 2 * distance + 1, :],
        scale_ref[2 * distance + 1 : 2 * distance + 2, :],
    )


def fold_max(block):
    top = block[0:8]
    for at in range(8, block.shape[0], 8):
        top = jnp.maximum(top, block[at : at + 8])
    return top


def scores_of(key_block, q_ref, head):
    q = q_ref[:, head * HD : (head + 1) * HD]
    return lax.dot_general(key_block, q, (((1,), (1,)), ((), ())), preferred_element_type=jnp.float32)


def cache_scores(keys_ref, q_ref, head, at):
    return scores_of(keys_ref[at : at + CHUNK, :], q_ref, head)


def fill_keys(k_ref, spare_ref, live, keys_ref):
    keys = k_ref[...].astype(jnp.float32)
    spare = jnp.where(live[:, :HD] > 0, keys[0:1], spare_ref[0:1, :].astype(jnp.float32))
    slot = lax.broadcasted_iota(jnp.int32, keys.shape, 0)
    keys_ref[...] = jnp.where(slot < live[:, :HD], keys, spare).astype(jnp.bfloat16)


def fill_values(v_ref, vt_ref, live=None):
    slots = v_ref.shape[0]
    values = v_ref[...]
    ones = jnp.ones((ONES_ROWS, slots), jnp.float32)
    if live is not None:
        slot = lax.broadcasted_iota(jnp.int32, values.shape, 0)
        values = jnp.where(slot < live[:, :HD], values.astype(jnp.float32), 0.0).astype(jnp.bfloat16)
        lane = lax.broadcasted_iota(jnp.int32, ones.shape, 1)
        ones = jnp.where(lane < jnp.concatenate([live[:, :HD]] * (slots // HD), axis=1), ones, 0.0)
    vt_ref[:HD, :] = values.T
    vt_ref[HD:, :] = ones.astype(jnp.bfloat16)


def prepare_kernel(
    counts_hbm, exps_hbm, q_hbm, nk_hbm, nv_hbm, k_hbm, v_hbm,
    q_ref, live_ref, scale_ref, nk_ref, keys_ref, vt_ref, nvt_ref,
    counts_ref, exps_ref, nv_ref, k_ref, v_ref, sems,
):
    pairs = (
        (counts_hbm, counts_ref), (exps_hbm, exps_ref), (nk_hbm, nk_ref), (k_hbm, k_ref),
        (nv_hbm, nv_ref), (v_hbm, v_ref), (q_hbm, q_ref),
    )
    copies = [pltpu.make_async_copy(source, target, sems.at[n]) for n, (source, target) in enumerate(pairs)]
    for copy in copies:
        copy.start()
    for copy in copies:
        copy.wait()
    facts = [cache_facts(counts_ref, exps_ref, distance, q_ref.shape[0]) for distance in range(3)]
    for distance, (live, factor, value_scale) in enumerate(facts):
        live_ref[distance : distance + 1, :] = live
        scale_ref[2 * distance : 2 * distance + 1, :] = factor
        scale_ref[2 * distance + 1 : 2 * distance + 2, :] = value_scale
    fill_keys(k_ref, nk_ref, facts[0][0], keys_ref)
    fill_values(nv_ref, nvt_ref)
    fill_values(v_ref, vt_ref, facts[0][0])


def near_kernel(
    q_ref, live_ref, scale_ref, nk_ref, keys_ref, vt_ref, nvt_ref, far_k_ref, far_v_ref,
    acc_ref, peak_ref, total_ref,
    far_keys_ref, far_vt_ref, s_ref, far_s_ref, n_ref, p_ref, far_p_ref, pn_ref,
):
    rows = q_ref.shape[0]
    slots = far_k_ref.shape[0]
    facts = [facts_at(live_ref, scale_ref, distance) for distance in range(2)]
    fill_keys(far_k_ref, nk_ref, facts[1][0], far_keys_ref)
    fill_values(far_v_ref, far_vt_ref, facts[1][0])
    caches = (
        (keys_ref, vt_ref, s_ref, p_ref) + facts[0][1:],
        (far_keys_ref, far_vt_ref, far_s_ref, far_p_ref) + facts[1][1:],
    )

    def scores(head, slot):
        key = lax.broadcasted_iota(jnp.int32, (rows, rows), 0)
        row = lax.broadcasted_iota(jnp.int32, (rows, rows), 1)
        fresh = jnp.where(key <= row, scores_of(nk_ref[...], q_ref, head), MASKED)
        n_ref[slot] = fresh
        top = fold_max(fresh) * BASE_FACTOR
        for keys, _, kept_scores, _, factor, _ in caches:
            for at in range(0, slots, CHUNK):
                cached = cache_scores(keys, q_ref, head, at)
                kept_scores[slot, at : at + CHUNK, :] = cached
                top = jnp.maximum(top, fold_max(cached) * factor)
        return top

    top = scores(0, 0)
    for head in range(GROUP):
        slot = head % 2
        peak = jnp.max(top, axis=0, keepdims=True)
        if head + 1 < GROUP:
            top = scores(head + 1, 1 - slot)
        pn_ref[slot] = jnp.exp2(n_ref[slot] * BASE_FACTOR - peak).astype(jnp.bfloat16)
        summed = jnp.dot(nvt_ref[...], pn_ref[slot], preferred_element_type=jnp.float32)
        acc, total = summed[:HD], summed[HD : HD + 1]
        for _, values, kept_scores, weights, factor, value_scale in caches:
            for at in range(0, slots, CHUNK):
                weights[slot, at : at + CHUNK, :] = jnp.exp2(
                    kept_scores[slot, at : at + CHUNK, :] * factor - peak
                ).astype(jnp.bfloat16)
            summed = jnp.dot(values[...], weights[slot], preferred_element_type=jnp.float32)
            acc += value_scale * summed[:HD]
            total += summed[HD : HD + 1]
        acc_ref[head * HD : (head + 1) * HD, :] = acc
        total_ref[head : head + 1, :] = total
        peak_ref[head : head + 1, :] = peak


def last_weights_kernel(
    live_ref, scale_ref, q_ref, nk_ref, k_ref, peak_in, weights_ref, kept_ref, s_ref, keys_ref, *, distance
):
    slots = k_ref.shape[0]
    live, factor, _ = facts_at(live_ref, scale_ref, distance)
    fill_keys(k_ref, nk_ref, live, keys_ref)

    def scores(head, slot):
        top = None
        for at in range(0, slots, CHUNK):
            cached = cache_scores(keys_ref, q_ref, head, at)
            s_ref[slot, at : at + CHUNK, :] = cached
            top = fold_max(cached) if top is None else jnp.maximum(top, fold_max(cached))
        return top

    top = scores(0, 0)
    for head in range(GROUP):
        slot = head % 2
        before = peak_in[head : head + 1, :]
        peak = jnp.maximum(before, jnp.max(top, axis=0, keepdims=True) * factor)
        kept_ref[head : head + 1, :] = jnp.exp2(before - peak)
        if head + 1 < GROUP:
            top = scores(head + 1, 1 - slot)
        for at in range(0, slots, CHUNK):
            weights_ref[head * slots + at : head * slots + at + CHUNK, :] = jnp.exp2(
                s_ref[slot, at : at + CHUNK, :] * factor - peak
            ).astype(jnp.bfloat16)


def row_plan(head_axis):
    index = lax.axis_index(head_axis)
    chip, core = index // 2, index % 2
    one, three = chip + 1 - 2 * (chip % 2), 3 - chip
    first = jnp.where(core == 0, one, three)
    second = jnp.where(core == 0, three, one)
    opposite = 3 - one
    return chip, core, first, second, opposite


def split_rows(turned_ref, send_ref, keep_ref):
    chip, core, first, second, opposite = row_plan("head")
    block = turned_ref.shape[0] // 8
    for out_ref, owner_core, chips in (
        (send_ref, 1 - core, (chip, first, second, opposite)),
        (keep_ref, core, (chip, second, first, opposite)),
    ):
        for at, owner in enumerate(chips):
            start = pl.multiple_of((2 * owner + owner_core) * block, block)
            out_ref[at * block : (at + 1) * block, :] = turned_ref[pl.ds(start, block), :]


def finish_kernel(
    live_ref, scale_ref, weights_ref, v_ref, acc_ref, kept_ref, total_ref,
    send_ref, keep_ref, vt_ref, turned_ref, *, distance,
):
    slots = v_ref.shape[0]
    live, _, value_scale = facts_at(live_ref, scale_ref, distance)
    fill_values(v_ref, vt_ref, live)
    for head in range(GROUP):
        summed = jnp.dot(
            vt_ref[...], weights_ref[head * slots : (head + 1) * slots, :],
            preferred_element_type=jnp.float32,
        )
        at = slice(head * HD, (head + 1) * HD)
        kept = kept_ref[head : head + 1, :]
        total = total_ref[head : head + 1, :] * kept + summed[HD : HD + 1]
        attended = (acc_ref[at, :] * kept + value_scale * summed[:HD]) / total
        turned_ref[:, at] = attended.T.astype(jnp.bfloat16)
    split_rows(turned_ref, send_ref, keep_ref)


def project_own_kernel(keep_ref, w_ref, out_ref):
    step = 512
    for at in range(0, out_ref.shape[1], step):
        columns = slice(at, at + step)
        out_ref[:, columns] = jnp.dot(keep_ref[...], w_ref[:, columns], preferred_element_type=jnp.float32)


def project_kernel(own_ref, got_ref, other_w_ref, send_out, keep_out, *, start):
    half, width = keep_out.shape
    step = 512
    for at in range(0, width, step):
        columns = slice(start + at, start + at + step)
        partial = own_ref[:, columns] + jnp.dot(
            got_ref[...], other_w_ref[:, columns], preferred_element_type=jnp.float32
        )
        keep_out[:, at : at + step] = partial[:half]
        send_out[:, at : at + step] = partial[half:].astype(jnp.bfloat16)


def params(mib):
    return pltpu.CompilerParams(vmem_limit_bytes=mib << 20)


def cost(keys, rows, products):
    wide = GROUP * rows * keys
    return pl.CostEstimate(flops=2 * products * wide * HD, transcendentals=wide, bytes_accessed=1 << 20)


def shifted(value, axis, steps):
    count = lax.axis_size(axis)
    return lax.ppermute(value, axis, [(i, i + steps) for i in range(count - steps)])


def core_pairs():
    return [(i, i ^ 1) for i in range(8)]


def chip_pairs(first):
    pairs = []
    for i in range(8):
        chip, core = i // 2, i % 2
        other = chip ^ 1 if (core == 0) == first else chip ^ 3
        pairs.append((i, 2 * other + core))
    return pairs


def on_device(
    queries, new_keys, new_values, cache_keys, cache_values, key_counts, scale_exps, out_weight
):
    rows = queries.shape[0]
    own_keys = cache_keys[0, 0]
    own_values = cache_values[0, 0]
    slots = own_keys.shape[0]
    exps = scale_exps.T
    wide = GROUP * HD
    f32, bf16 = jnp.float32, jnp.bfloat16

    keys_1 = shifted(own_keys, "section", 1)
    values_1 = shifted(own_values, "section", 1)
    other_weight = lax.ppermute(out_weight, "head", core_pairs())
    keys_2 = shifted(keys_1, "section", 1)
    values_2 = shifted(values_1, "section", 1)

    acc_shape = jax.ShapeDtypeStruct((wide, rows), f32)
    row_shape = jax.ShapeDtypeStruct((GROUP, rows), f32)
    vt = lambda n: pltpu.VMEM((HD + ONES_ROWS, n), bf16)
    pair = lambda n, t: pltpu.VMEM((2, n, rows), t)
    local = (key_counts, exps, queries, new_keys, new_values, own_keys, own_values)
    like = lambda *shape: jax.ShapeDtypeStruct(shape, bf16)
    ready = pl.pallas_call(
        prepare_kernel,
        out_shape=(
            like(*queries.shape), jax.ShapeDtypeStruct((GROUP, rows), jnp.int32), row_shape,
            like(*new_keys.shape), like(*own_keys.shape), like(HD + ONES_ROWS, slots), like(HD + ONES_ROWS, rows),
        ),
        in_specs=[HBM] * 7,
        out_specs=(VMEM,) * 7,
        scratch_shapes=[
            pltpu.SMEM(key_counts.shape, jnp.int32), pltpu.SMEM(exps.shape, jnp.int32),
            pltpu.VMEM(new_values.shape, bf16), pltpu.VMEM(own_keys.shape, bf16),
            pltpu.VMEM(own_values.shape, bf16), pltpu.SemaphoreType.DMA((7,)),
        ],
        compiler_params=params(8),
        cost_estimate=pl.CostEstimate(flops=1 << 20, transcendentals=0, bytes_accessed=1 << 20),
        name="prepare",
    )(*(pltpu.with_memory_space_constraint(value, pltpu.HBM) for value in local))
    q, live, scale, near_keys = ready[:4]
    acc, peak, total = pl.pallas_call(
        near_kernel,
        out_shape=(acc_shape, row_shape, row_shape),
        in_specs=[VMEM] * 9,
        out_specs=(VMEM,) * 3,
        scratch_shapes=[
            pltpu.VMEM(own_keys.shape, bf16), vt(slots),
            pair(slots, f32), pair(slots, f32), pair(rows, f32),
            pair(slots, bf16), pair(slots, bf16), pair(rows, bf16),
        ],
        compiler_params=params(24),
        cost_estimate=cost(2 * slots + rows, rows, 2),
        name="near",
    )(*ready, keys_1, values_1)
    weights, kept = pl.pallas_call(
        functools.partial(last_weights_kernel, distance=2),
        out_shape=(jax.ShapeDtypeStruct((GROUP * slots, rows), bf16), row_shape),
        in_specs=[VMEM] * 6,
        out_specs=(VMEM, VMEM),
        scratch_shapes=[pair(slots, f32), pltpu.VMEM(own_keys.shape, bf16)],
        compiler_params=params(16),
        cost_estimate=cost(slots, rows, 1),
        name="last",
    )(live, scale, q, near_keys, keys_2, peak)

    half, quarter, eighth = rows // 2, rows // 4, rows // 8
    send, keep = pl.pallas_call(
        functools.partial(finish_kernel, distance=2),
        out_shape=(jax.ShapeDtypeStruct((half, wide), bf16),) * 2,
        in_specs=[VMEM] * 7,
        out_specs=(VMEM, VMEM),
        scratch_shapes=[vt(slots), pltpu.VMEM((rows, wide), bf16)],
        compiler_params=params(16),
        cost_estimate=cost(slots, rows, 1),
        name="finish",
    )(live, scale, weights, values_2, acc, kept, total)
    got = lax.ppermute(send, "head", core_pairs())
    own_share = pl.pallas_call(
        project_own_kernel,
        out_shape=jax.ShapeDtypeStruct((half, out_weight.shape[1]), f32),
        in_specs=[VMEM] * 2,
        out_specs=VMEM,
        compiler_params=params(16),
        cost_estimate=pl.CostEstimate(
            flops=2 * half * wide * out_weight.shape[1], transcendentals=0, bytes_accessed=1 << 20
        ),
        name="project_own",
    )(keep, out_weight)

    width = out_weight.shape[1]
    cut = 3 * width // 8
    size = lax.axis_size("section")
    pieces = []
    for start, part in ((0, cut), (cut, width - cut)):
        send, kept_rows = pl.pallas_call(
            functools.partial(project_kernel, start=start),
            out_shape=(jax.ShapeDtypeStruct((quarter, part), bf16), jax.ShapeDtypeStruct((quarter, part), f32)),
            in_specs=[VMEM] * 3,
            out_specs=(VMEM, VMEM),
            compiler_params=params(16),
            cost_estimate=pl.CostEstimate(
                flops=rows * wide * part, transcendentals=0, bytes_accessed=1 << 20
            ),
            name="project",
        )(own_share, got, other_weight)
        first = lax.ppermute(send, "head", chip_pairs(True))
        two = kept_rows + first.astype(f32)
        second = lax.ppermute(two[eighth:].astype(bf16), "head", chip_pairs(False))
        done = (two[:eighth] + second.astype(f32)).astype(bf16)
        pieces.append(lax.ppermute(done, "section", [(i, (i + 1) % size) for i in range(size)]))
    return jnp.concatenate(pieces, axis=1).astype(f32)


def solution(mesh):
    in_specs = (
        P("section", "head"),
        P("section", "head"),
        P("section", "head"),
        P("section", "head", None, None),
        P("section", "head", None, None),
        P(),
        P(),
        P("head", None),
    )
    out_specs = P(("section", "head"), None)
    return jax.shard_map(on_device, mesh=mesh, in_specs=in_specs, out_specs=out_specs, check_vma=False)
```
